32 devices in a mesh: ev: 8 (over y, x, core), st: 4 (over z).
Axes of the slice: x: 2, y: 2, z: 4, core: 2. Of those that a mesh axis runs over, the one named last changes fastest.
Arguments:
- amplitudes: bfloat16 [131072, 2048], P(('ev', 'st')), may hold values from -6 to 6
- event_mass: float32 [131072], P(('ev', 'st')), may hold values from 0.8 to 2.5
- data_rows: int32 [32], P(('ev', 'st')), may hold values from 256 to 2560, as said below
- wave_shape: int32 [1024], replicated, may hold values from 0 to 31
- pole_mass: float32 [32], replicated, may hold values from 1 to 2.3
- pole_width: float32 [32], replicated, may hold values from 0.1 to 0.5
- coefficients: float32 [128, 2048], replicated, may hold values from -6 to 6
- background: float32 [128], replicated, may hold values from 0.2 to 2
Outputs:
- gradient: float32 [128, 2048], P('st')
- likelihood: float32 [128], P('st')
The draws below stay inside these ranges and needn't reach their ends.
Inputs may be any that keep to these rules, and one draw needn't show every extreme that they name: `data_rows`: each device holds its data events first; the share of data events differs strongly from device to device.
All inputs are finite; a program needn't handle non-finite values.
Results may differ from the reference program's by a relative error of at most 0.0032.
Values sent between devices are 32-bit elements; how exact they have to be, the bound alone decides.
A program may use at most 64 MiB of HBM per device.

```python
import math
import jax
import jax.numpy as jnp
from jax import lax

W = 1024
STARTS = 128
SHAPES = 32
EV_DEV = 4096
EVENTS = 131072
DEVICES = 32


def draw_data_rows(key, part):
    position = jnp.arange(DEVICES, dtype=jnp.int32)
    rising = position * (EV_DEV // 2) // max(DEVICES - 1, 1)
    jitter = jax.random.randint(jax.random.fold_in(key, 17), (DEVICES,), 0, EV_DEV // 16 + 1, dtype=jnp.int32)
    return (EV_DEV // 16 + rising + jitter).astype(jnp.int32)


def plant(drawn, rng, low, largest):
    longest = drawn.shape.index(max(drawn.shape))
    spots = []
    for shift in (0, 1):
        where = [jax.random.randint(jax.random.fold_in(rng, axis), (), 0, length) for axis, length in enumerate(drawn.shape)]
        where[longest] = (where[longest] + shift) % drawn.shape[longest]
        spots.append(tuple(where))
    return drawn.at[spots[0]].set(low).at[spots[1]].set(largest)


def level_of(stream_key, shape, shards, low, high):
    factor_of, own = 1.0, jax.random.fold_in(stream_key, 6)
    for dim, parts in shards:
        steps = jnp.exp(jax.random.uniform(jax.random.fold_in(own, dim), (parts,), jnp.float32, low / len(shards), high / len(shards)))
        factor_of = factor_of * jnp.repeat(steps, shape[dim] // parts).reshape([-1 if axis == dim else 1 for axis in range(len(shape))])
    return factor_of


def normal_values(key, extent, scale, bound, cuts=(), kind=jnp.bfloat16):
    drawn = jax.random.normal(key, extent, jnp.float32) * scale
    if len(cuts) > 0:
        drawn = level_of(key, extent, cuts, -0.22, 0.18) * drawn
    return jnp.clip(drawn, min=-bound, max=bound).astype(kind)


def setup_inputs(seed: int = 0) -> dict:
    seeds = jax.random.split(jax.random.key(seed), 9)
    return {
        "amplitudes": normal_values(seeds[0], (EVENTS, 2 * W), 1.0, 6.0, ((0, 32),)),
        "event_mass": jnp.clip(0.8 + 1.7 * jax.random.uniform(seeds[1], (EVENTS,), jnp.float32) ** level_of(seeds[1], (EVENTS,), ((0, 32),), -0.2, 0.2), 0.8, 2.5),
        "data_rows": draw_data_rows(jax.random.fold_in(seeds[8], 71), 0),
        "wave_shape": plant(jax.random.randint(seeds[3], (W,), 0, SHAPES), jax.random.fold_in(seeds[3], 1), 0, SHAPES - 1).astype(jnp.int32),
        "pole_mass": jnp.clip(jax.random.uniform(seeds[4], (SHAPES,), jnp.float32, 1.0, 2.3), 1.0, 2.3),
        "pole_width": jnp.clip(jax.random.uniform(seeds[5], (SHAPES,), jnp.float32, 0.1, 0.5), 0.1, 0.5),
        "coefficients": normal_values(seeds[6], (STARTS, 2 * W), 1.0, 6.0, (), jnp.float32),
        "background": jnp.clip(jnp.exp(jax.random.uniform(seeds[7], (STARTS,), jnp.float32, math.log(0.2), math.log(2.0))), 0.2, 2.0),
    }


def fold_parts(block):
    half_s = block.shape[0] // 2
    half_w = block.shape[1] // 2
    real_part = block[:half_s, :half_w] + block[half_s:, half_w:]
    imag_part = block[half_s:, :half_w] - block[:half_s, half_w:]
    return jnp.concatenate([real_part, imag_part], 1)


def reference(amplitudes, event_mass, data_rows, wave_shape, pole_mass, pole_width, coefficients, background):
    coef = coefficients.astype(jnp.bfloat16)
    coef_real = coef[:, :W].T
    coef_imag = coef[:, W:].T
    mixing = jnp.concatenate([jnp.concatenate([coef_real, coef_imag], 1), jnp.concatenate([-coef_imag, coef_real], 1)], 0)
    selector = wave_shape[None, :] == jnp.arange(SHAPES, dtype=jnp.int32)[:, None]
    peak = pole_mass * pole_width
    square = pole_mass * pole_mass
    wave_peak = jnp.sum(jnp.where(selector, peak[:, None], 0.0), 0)
    wave_peak2 = jnp.sum(jnp.where(selector, (peak * peak)[:, None], 0.0), 0)
    wave_square = jnp.sum(jnp.where(selector, square[:, None], 0.0), 0)
    scale = W ** -0.5

    def device_step(carry, inputs):
        grads, log_sum, sim_sum = carry
        piece, mass, limit = inputs
        offset = wave_square[None, :] - (mass * mass)[:, None]
        denom = offset * offset + wave_peak2[None, :]
        wide_real = wave_peak[None, :] * offset / denom
        wide_imag = wave_peak2[None, :] / denom
        amp_real = piece[:, :W].astype(jnp.float32)
        amp_imag = piece[:, W:].astype(jnp.float32)
        dressed = jnp.concatenate([amp_real * wide_real - amp_imag * wide_imag, amp_real * wide_imag + amp_imag * wide_real], 1).astype(jnp.bfloat16)
        value = jnp.dot(dressed, mixing, preferred_element_type=jnp.float32) * scale
        val_real = value[:, :STARTS]
        val_imag = value[:, STARTS:]
        intensity = val_real * val_real + val_imag * val_imag + background[None, :]
        is_data = (jnp.arange(EV_DEV, dtype=jnp.int32) < limit)[:, None]
        log_sum = log_sum + jnp.sum(jnp.where(is_data, jnp.log(intensity), 0.0), 0)
        sim_sum = sim_sum + jnp.sum(jnp.where(is_data, 0.0, intensity), 0)
        factor = jnp.where(is_data, -1.0 / intensity, 1.0)
        weighted = (2.0 * jnp.concatenate([factor, factor], 1) * value).astype(jnp.bfloat16)
        nothing = jnp.zeros_like(weighted)
        split = jnp.concatenate([jnp.where(is_data, weighted, nothing), jnp.where(is_data, nothing, weighted)], 1)
        grads = grads + jnp.dot(split.T, dressed, preferred_element_type=jnp.float32)
        return (grads, log_sum, sim_sum), None

    start = (jnp.zeros((4 * STARTS, 2 * W), jnp.float32), jnp.zeros((STARTS,), jnp.float32), jnp.zeros((STARTS,), jnp.float32))
    inputs = (amplitudes.reshape(DEVICES, EV_DEV, 2 * W), event_mass.reshape(DEVICES, EV_DEV), data_rows)
    (grads, log_sum, sim_sum), _ = lax.scan(device_step, start, inputs)
    n_data = jnp.sum(data_rows.astype(jnp.float32))
    n_sim = EVENTS - n_data
    data_part = fold_parts(grads[:2 * STARTS]) * scale
    sim_part = fold_parts(grads[2 * STARTS:]) * scale
    gradient = W * (data_part / n_data + sim_part / n_sim)
    likelihood = -log_sum / n_data + sim_sum / n_sim
    return gradient, likelihood
```

```python
import functools

import jax
import jax.numpy as jnp
from jax import lax
from jax.experimental import pallas as pl
from jax.experimental.pallas import tpu as pltpu
from jax.sharding import PartitionSpec as P

BLOCK = 512
ROWS = 16
LANES = 256
MESH = pl.DeviceIdType.MESH
F32 = jnp.float32
BF16 = jnp.bfloat16


def compute_kernel(
    limit_ref,
    pole_mass_ref,
    pole_width_ref,
    amp_ref,
    mass_ref,
    wave_ref,
    coef_ref,
    back_ref,
    grad_ref,
    sums_ref,
    mix,
    square,
    inverse,
    mass2,
    dressed,
    acc,
):
    step = pl.program_id(0)
    steps = pl.num_programs(0)
    waves = wave_ref.shape[1]
    starts = back_ref.shape[1]
    scale = waves ** (-0.5)
    limit = limit_ref[0]
    first = step * BLOCK

    @pl.when(step == 0)
    def _():
        which = wave_ref[...]
        peak = jnp.zeros(which.shape, F32)
        center = jnp.zeros(which.shape, F32)
        for k in range(pole_mass_ref.shape[0]):
            mass_k = pole_mass_ref[k]
            peak = jnp.where(which == k, mass_k * pole_width_ref[k], peak)
            center = jnp.where(which == k, mass_k * mass_k, center)
        square[...] = jnp.broadcast_to(center, square.shape)
        inverse[...] = jnp.broadcast_to(1.0 / peak, inverse.shape)
        coef_real = coef_ref[:, :waves].T
        coef_imag = coef_ref[:, waves:].T
        mix[:waves, :starts] = coef_real.astype(BF16)
        mix[:waves, starts:] = coef_imag.astype(BF16)
        mix[waves:, :starts] = (-coef_imag).astype(BF16)
        mix[waves:, starts:] = coef_real.astype(BF16)
        acc[...] = jnp.zeros_like(acc)
        sums_ref[...] = jnp.zeros_like(sums_ref)

    mass = mass_ref[0]
    mass2[...] = jnp.broadcast_to(mass * mass, (128, BLOCK)).T

    def dress(index, carry):
        row = pl.multiple_of(index * ROWS, ROWS)
        here = pl.ds(row, ROWS)
        m2 = mass2[here, :]
        m2 = jnp.concatenate([m2] * (LANES // 128), 1)
        for col in range(0, waves, LANES):
            real_cols = pl.ds(col, LANES)
            imag_cols = pl.ds(waves + col, LANES)
            sq = square[:, real_cols]
            inv = inverse[:, real_cols]
            sq = jnp.concatenate([sq] * (ROWS // 8), 0)
            inv = jnp.concatenate([inv] * (ROWS // 8), 0)
            u = (sq - m2) * inv
            denom = u * u + 1.0
            guess = pl.reciprocal(denom, approx=True)
            r = guess * (2.0 - denom * guess)
            amp_real = amp_ref[here, real_cols].astype(F32)
            amp_imag = amp_ref[here, imag_cols].astype(F32)
            dressed[here, real_cols] = ((amp_real * u - amp_imag) * r).astype(BF16)
            dressed[here, imag_cols] = ((amp_imag * u + amp_real) * r).astype(BF16)
        return carry

    lax.fori_loop(0, BLOCK // ROWS, dress, 0)

    value = jnp.dot(dressed[...], mix[...], preferred_element_type=F32) * scale
    val_real = value[:, :starts]
    val_imag = value[:, starts:]
    intensity = val_real * val_real + val_imag * val_imag + back_ref[...]
    is_data = first + lax.broadcasted_iota(jnp.int32, (BLOCK, starts), 0) < limit
    log_part = jnp.sum(jnp.where(is_data, jnp.log(intensity), 0.0), 0, keepdims=True)
    sim_part = jnp.sum(jnp.where(is_data, 0.0, intensity), 0, keepdims=True)
    sums_ref[0:1, :] += log_part
    sums_ref[1:2, :] += sim_part
    factor = jnp.where(is_data, -2.0 / intensity, 2.0)
    weighted = jnp.concatenate([factor * val_real, factor * val_imag], 1)
    both = jnp.concatenate([is_data, is_data], 1)

    @pl.when(first < limit)
    def _():
        w = jnp.where(both, weighted, 0.0).T.astype(BF16)
        acc[0] += jnp.dot(w, dressed[...], preferred_element_type=F32)

    @pl.when(first + BLOCK > limit)
    def _():
        w = jnp.where(both, 0.0, weighted).T.astype(BF16)
        acc[1] += jnp.dot(w, dressed[...], preferred_element_type=F32)

    @pl.when(step == steps - 1)
    def _():
        for part in range(2):
            grad_ref[part, :, :waves] = acc[part, :starts, :waves] + acc[part, starts:, waves:]
            grad_ref[part, :, waves:] = acc[part, starts:, :waves] - acc[part, :starts, waves:]


def compute(amplitudes, event_mass, data_rows, wave_shape, pole_mass, pole_width, coefficients, background):
    rows, wide = amplitudes.shape
    waves = wide // 2
    starts = coefficients.shape[0]
    smem = pl.BlockSpec(memory_space=pltpu.SMEM)
    return pl.pallas_call(
        compute_kernel,
        grid=(rows // BLOCK,),
        in_specs=[
            smem,
            smem,
            smem,
            pl.BlockSpec((BLOCK, wide), lambda i: (i, 0)),
            pl.BlockSpec((1, 1, BLOCK), lambda i: (i, 0, 0)),
            pl.BlockSpec((1, waves), lambda i: (0, 0)),
            pl.BlockSpec((starts, wide), lambda i: (0, 0)),
            pl.BlockSpec((1, starts), lambda i: (0, 0)),
        ],
        out_specs=[
            pl.BlockSpec((2, starts, wide), lambda i: (0, 0, 0)),
            pl.BlockSpec((8, starts), lambda i: (0, 0)),
        ],
        out_shape=[
            jax.ShapeDtypeStruct((2, starts, wide), F32),
            jax.ShapeDtypeStruct((8, starts), F32),
        ],
        scratch_shapes=[
            pltpu.VMEM((wide, 2 * starts), BF16),
            pltpu.VMEM((8, waves), F32),
            pltpu.VMEM((8, waves), F32),
            pltpu.VMEM((BLOCK, 128), F32),
            pltpu.VMEM((BLOCK, wide), BF16),
            pltpu.VMEM((2, 2 * starts, wide), F32),
        ],
        compiler_params=pltpu.CompilerParams(
            dimension_semantics=("arbitrary",), vmem_limit_bytes=48 * 1024 * 1024
        ),
        name="dress_and_fit",
    )(
        data_rows,
        pole_mass,
        pole_width,
        amplitudes,
        event_mass.reshape(rows // BLOCK, 1, BLOCK),
        wave_shape.reshape(1, waves),
        coefficients,
        background.reshape(1, starts),
    )


def reduce_kernel(
    n_ev,
    n_st,
    events,
    count_ref,
    grad_ref,
    sums_ref,
    out_ref,
    like_ref,
    tell,
    heard,
    mine,
    core_in,
    plane_sum,
    plane_in,
    st_sum,
    st_in,
    done,
    done_in,
    tell_send,
    tell_recv,
    core_send,
    core_recv,
    plane_send,
    plane_recv,
    st_send,
    st_recv,
    done_send,
    done_recv,
):
    ev = lax.axis_index("ev")
    st = lax.axis_index("st")
    n_dev = n_ev * n_st
    planes = n_ev // 2
    core = lax.rem(ev, 2)
    plane = ev // 2
    me = ev * n_st + st
    starts, wide = grad_ref.shape[1:]
    waves = wide // 2
    group = starts // n_st
    width = mine.shape[-1]
    chunks = wide // width

    def peer(offset):
        other = lax.rem(me + offset, n_dev)
        return other // n_st, lax.rem(other, n_st)

    barrier = pltpu.get_barrier_semaphore()
    for offset in range(1, n_dev):
        pl.semaphore_signal(barrier, inc=1, device_id=peer(offset), device_id_type=MESH)

    lane = lax.broadcasted_iota(jnp.int32, (1, 128), 1)
    count = jnp.full((1, 128), count_ref[0], jnp.int32).astype(F32)
    logs = sums_ref[0:1, :]
    sims = sums_ref[1:2, :]
    for z in range(n_st):
        log_row = pltpu.roll(logs, (128 - z * group) % 128, 1) if z else logs
        sim_row = pltpu.roll(sims, (128 + group - z * group) % 128, 1)
        row = jnp.where(lane < group, log_row, jnp.where(lane < 2 * group, sim_row, count))
        tell[z, 0:1, :] = row

    pl.semaphore_wait(barrier, n_dev - 1)

    told = []
    for offset in range(1, n_dev):
        to_ev, to_st = peer(offset)
        copy = pltpu.make_async_remote_copy(
            src_ref=tell.at[to_st, pl.ds(0, 1), :],
            dst_ref=heard.at[me, pl.ds(0, 1), :],
            send_sem=tell_send.at[offset],
            recv_sem=tell_recv.at[me],
            device_id=(to_ev, to_st),
            device_id_type=MESH,
        )
        copy.start()
        told.append(copy)
    heard[me, 0:1, :] = tell[st, 0:1, :]
    for offset in range(1, n_dev):
        from_me = lax.rem(me + offset, n_dev)
        pltpu.make_async_remote_copy(
            src_ref=tell.at[0, pl.ds(0, 1), :],
            dst_ref=heard.at[from_me, pl.ds(0, 1), :],
            send_sem=tell_send.at[offset],
            recv_sem=tell_recv.at[from_me],
            device_id=peer(offset),
            device_id_type=MESH,
        ).wait_recv()
    total = heard[0, 0:1, :]
    for index in range(1, n_dev):
        total = total + heard[index, 0:1, :]
    n_data = jnp.sum(jnp.where(lane == 2 * group, total, 0.0), 1, keepdims=True)
    n_sim = events - n_data
    like_ref[...] = pltpu.roll(total, 128 - group, 1) / n_sim - total / n_data
    scale = waves ** 0.5
    by_data = jnp.broadcast_to(scale / n_data, (8, width))
    by_sim = jnp.broadcast_to(scale / n_sim, (8, width))

    def place(index):
        return 8 * (index // chunks), width * (index % chunks)

    for c in range(2):
        for p in range(planes):
            row, col = place(c * planes + p)
            for z in range(n_st):
                here = (pl.ds(z * group + row, 8), pl.ds(col, width))
                mine[c, p, z] = (
                    grad_ref[(0, *here)] * by_data + grad_ref[(1, *here)] * by_sim
                )

    first = pltpu.make_async_remote_copy(
        src_ref=mine.at[1 - core],
        dst_ref=core_in,
        send_sem=core_send,
        recv_sem=core_recv,
        device_id=(2 * plane + 1 - core, st),
        device_id_type=MESH,
    )
    first.start()
    first.wait_recv()
    plane_sum[...] = mine[core] + core_in[...]

    plane_copies = []
    for offset in range(1, planes):
        to = lax.rem(plane + offset, planes)
        copy = pltpu.make_async_remote_copy(
            src_ref=plane_sum.at[to],
            dst_ref=plane_in.at[offset],
            send_sem=plane_send.at[offset],
            recv_sem=plane_recv.at[offset],
            device_id=(2 * to + core, st),
            device_id_type=MESH,
        )
        copy.start()
        plane_copies.append(copy)
    part = plane_sum[plane]
    for offset in range(1, planes):
        plane_copies[offset - 1].wait_recv()
        part = part + plane_in[offset]
    st_sum[...] = part

    st_copies = []
    for offset in range(1, n_st):
        to = lax.rem(st + offset, n_st)
        copy = pltpu.make_async_remote_copy(
            src_ref=st_sum.at[to],
            dst_ref=st_in.at[offset],
            send_sem=st_send.at[offset],
            recv_sem=st_recv.at[offset],
            device_id=(ev, to),
            device_id_type=MESH,
        )
        copy.start()
        st_copies.append(copy)
    part = st_sum[st]
    for offset in range(1, n_st):
        st_copies[offset - 1].wait_recv()
        part = part + st_in[offset]
    done[...] = part

    slot = core * planes + plane
    done_copies = []
    for offset in range(1, n_ev):
        to = lax.rem(ev + offset, n_ev)
        copy = pltpu.make_async_remote_copy(
            src_ref=done,
            dst_ref=done_in.at[slot],
            send_sem=done_send.at[offset],
            recv_sem=done_recv.at[slot],
            device_id=(to, st),
            device_id_type=MESH,
        )
        copy.start()
        done_copies.append(copy)
    done_in[slot] = part
    for offset in range(1, n_ev):
        other = lax.rem(ev + offset, n_ev)
        other_slot = lax.rem(other, 2) * planes + other // 2
        pltpu.make_async_remote_copy(
            src_ref=done,
            dst_ref=done_in.at[other_slot],
            send_sem=done_send.at[offset],
            recv_sem=done_recv.at[other_slot],
            device_id=(other, st),
            device_id_type=MESH,
        ).wait_recv()
    for index in range(n_ev):
        row, col = place(index)
        out_ref[row : row + 8, col : col + width] = done_in[index]

    for copy in told + [first] + plane_copies + st_copies + done_copies:
        copy.wait_send()


def reduce_all(n_ev, n_st, events, data_rows, grads, sums):
    starts, wide = grads.shape[1:]
    group = starts // n_st
    planes = n_ev // 2
    width = group * wide // (8 * n_ev)
    n_dev = n_ev * n_st
    dma = pltpu.SemaphoreType.DMA
    vmem = pl.BlockSpec(memory_space=pltpu.VMEM)
    return pl.pallas_call(
        functools.partial(reduce_kernel, n_ev, n_st, events),
        in_specs=[pl.BlockSpec(memory_space=pltpu.SMEM), vmem, vmem],
        out_specs=[vmem, vmem],
        out_shape=[
            jax.ShapeDtypeStruct((group, wide), F32),
            jax.ShapeDtypeStruct((1, 128), F32),
        ],
        scratch_shapes=[
            pltpu.VMEM((n_st, 8, 128), F32),
            pltpu.VMEM((n_dev, 8, 128), F32),
            pltpu.VMEM((2, planes, n_st, 8, width), F32),
            pltpu.VMEM((planes, n_st, 8, width), F32),
            pltpu.VMEM((planes, n_st, 8, width), F32),
            pltpu.VMEM((planes, n_st, 8, width), F32),
            pltpu.VMEM((n_st, 8, width), F32),
            pltpu.VMEM((n_st, 8, width), F32),
            pltpu.VMEM((8, width), F32),
            pltpu.VMEM((n_ev, 8, width), F32),
            dma((n_dev,)),
            dma((n_dev,)),
            dma,
            dma,
            dma((planes,)),
            dma((planes,)),
            dma((n_st,)),
            dma((n_st,)),
            dma((n_ev,)),
            dma((n_ev,)),
        ],
        compiler_params=pltpu.CompilerParams(
            collective_id=0, has_side_effects=True, vmem_limit_bytes=32 * 1024 * 1024
        ),
        name="reduce_starts",
    )(data_rows, grads, sums)


def solution(mesh):
    n_ev = mesh.shape["ev"]
    n_st = mesh.shape["st"]

    def shards(
        amplitudes, event_mass, data_rows, wave_shape, pole_mass, pole_width, coefficients, background
    ):
        grads, sums = compute(
            amplitudes, event_mass, data_rows, wave_shape, pole_mass, pole_width, coefficients, background
        )
        events = amplitudes.shape[0] * n_ev * n_st
        gradient, like = reduce_all(n_ev, n_st, events, data_rows, grads, sums)
        return gradient, like[0, : coefficients.shape[0] // n_st]

    return jax.shard_map(
        shards,
        mesh=mesh,
        in_specs=(P(("ev", "st"), None), P(("ev", "st")), P(("ev", "st")), P(), P(), P(), P(), P()),
        out_specs=(P("st", None), P("st")),
        check_vma=False,
    )
```

```python
import functools

import jax
import jax.numpy as jnp
from jax import lax
from jax.experimental import pallas as pl
from jax.experimental.pallas import tpu as pltpu
from jax.sharding import PartitionSpec as P

BLOCK = 512
ROWS = 16
LANES = 256
MESH = pl.DeviceIdType.MESH
F32 = jnp.float32
BF16 = jnp.bfloat16


def fit_kernel(
    n_ev,
    n_st,
    parts,
    limit_hbm,
    pole_mass_hbm,
    pole_width_hbm,
    amp_hbm,
    mass_hbm,
    wave_hbm,
    coef_hbm,
    back_hbm,
    out_ref,
    like_ref,
    limit_ref,
    pole_mass_ref,
    pole_width_ref,
    amp_ref,
    mass_ref,
    wave_ref,
    coef_ref,
    back_ref,
    mix,
    square,
    inverse,
    mass2,
    sums,
    raw,
    weights,
    count_tell,
    count_heard,
    tell,
    heard,
    mine,
    core_in,
    plane_sum,
    plane_in,
    st_sum,
    st_in,
    done,
    done_in,
    load_sem,
    amp_sem,
    count_send,
    count_recv,
    tell_send,
    tell_recv,
    core_send,
    core_recv,
    plane_send,
    plane_recv,
    st_send,
    st_recv,
    done_send,
    done_recv,
):
    ev = lax.axis_index("ev")
    st = lax.axis_index("st")
    n_dev = n_ev * n_st
    planes = n_ev // 2
    core = lax.rem(ev, 2)
    plane = ev // 2
    me = ev * n_st + st
    rows, wide = amp_ref.shape
    waves = wide // 2
    starts = back_ref.shape[1]
    group = starts // n_st
    events = rows * n_dev
    blocks = rows // BLOCK
    scale = waves ** (-0.5)
    width = mine.shape[-1]
    part_waves = waves // parts
    per = 2 * part_waves // width

    def peer(offset):
        other = lax.rem(me + offset, n_dev)
        return other // n_st, lax.rem(other, n_st)

    loads = [
        pltpu.make_async_copy(src, dst, load_sem.at[index])
        for index, (src, dst) in enumerate(
            [
                (coef_hbm, coef_ref),
                (wave_hbm, wave_ref),
                (limit_hbm, limit_ref),
                (pole_mass_hbm, pole_mass_ref),
                (pole_width_hbm, pole_width_ref),
                (mass_hbm, mass_ref),
                (back_hbm, back_ref),
            ]
        )
    ]
    for load in loads:
        load.start()

    def fetch(index):
        here = pl.ds(pl.multiple_of(index * BLOCK, BLOCK), BLOCK)
        return pltpu.make_async_copy(amp_hbm.at[here, :], amp_ref.at[here, :], amp_sem.at[index])

    for index in range(blocks):
        fetch(index).start()

    barrier = pltpu.get_barrier_semaphore()
    for offset in range(1, n_dev):
        pl.semaphore_signal(barrier, inc=1, device_id=peer(offset), device_id_type=MESH)

    for load in loads:
        load.wait()
    limit = limit_ref[0]
    which = wave_ref[...]
    peak = jnp.zeros(which.shape, F32)
    center = jnp.zeros(which.shape, F32)
    for k in range(pole_mass_ref.shape[0]):
        mass_k = pole_mass_ref[k]
        peak = jnp.where(which == k, mass_k * pole_width_ref[k], peak)
        center = jnp.where(which == k, mass_k * mass_k, center)
    square[...] = jnp.broadcast_to(center, square.shape)
    inverse[...] = jnp.broadcast_to(1.0 / peak, inverse.shape)
    coef_real = coef_ref[:, :waves].T
    coef_imag = coef_ref[:, waves:].T
    mix[:waves, :starts] = coef_real.astype(BF16)
    mix[:waves, starts:] = coef_imag.astype(BF16)
    mix[waves:, :starts] = (-coef_imag).astype(BF16)
    mix[waves:, starts:] = coef_real.astype(BF16)
    sums[...] = jnp.zeros_like(sums)
    count_tell[0:1, :] = jnp.full((1, 128), limit, jnp.int32).astype(F32)

    pl.semaphore_wait(barrier, n_dev - 1)

    def count_copy(offset, slot):
        return pltpu.make_async_remote_copy(
            src_ref=count_tell.at[pl.ds(0, 1), :],
            dst_ref=count_heard.at[slot, pl.ds(0, 1), :],
            send_sem=count_send.at[offset],
            recv_sem=count_recv.at[slot],
            device_id=peer(offset),
            device_id_type=MESH,
        )

    for offset in range(1, n_dev):
        count_copy(offset, me).start()
    count_heard[me, 0:1, :] = count_tell[0:1, :]

    def block_step(step, carry):
        first = pl.multiple_of(step * BLOCK, BLOCK)
        fetch(step).wait()
        mass = mass_ref[step]
        mass2[...] = jnp.broadcast_to(mass * mass, (128, BLOCK)).T

        def dress(index, carry):
            row = pl.multiple_of(index * ROWS, ROWS)
            here = pl.ds(pl.multiple_of(first + row, ROWS), ROWS)
            m2 = mass2[pl.ds(row, ROWS), :]
            m2 = jnp.concatenate([m2] * (LANES // 128), 1)
            for col in range(0, waves, LANES):
                real_cols = pl.ds(col, LANES)
                imag_cols = pl.ds(waves + col, LANES)
                sq = jnp.concatenate([square[:, real_cols]] * (ROWS // 8), 0)
                inv = jnp.concatenate([inverse[:, real_cols]] * (ROWS // 8), 0)
                u = (sq - m2) * inv
                denom = u * u + 1.0
                guess = pl.reciprocal(denom, approx=True)
                r = guess * (2.0 - denom * guess)
                amp_real = amp_ref[here, real_cols].astype(F32)
                amp_imag = amp_ref[here, imag_cols].astype(F32)
                amp_ref[here, real_cols] = ((amp_real * u - amp_imag) * r).astype(BF16)
                amp_ref[here, imag_cols] = ((amp_imag * u + amp_real) * r).astype(BF16)
            return carry

        lax.fori_loop(0, BLOCK // ROWS, dress, 0)

        dressed = amp_ref[pl.ds(first, BLOCK), :]
        value = jnp.dot(dressed, mix[...], preferred_element_type=F32) * scale
        val_real = value[:, :starts]
        val_imag = value[:, starts:]
        intensity = val_real * val_real + val_imag * val_imag + back_ref[...]
        is_data = first + lax.broadcasted_iota(jnp.int32, (BLOCK, starts), 0) < limit
        sums[0:1, :] += jnp.sum(jnp.where(is_data, jnp.log(intensity), 0.0), 0, keepdims=True)
        sums[1:2, :] += jnp.sum(jnp.where(is_data, 0.0, intensity), 0, keepdims=True)
        factor = jnp.where(is_data, -2.0 / intensity, 2.0)
        raw[step] = jnp.concatenate([factor * val_real, factor * val_imag], 1).T
        return carry

    lax.fori_loop(0, blocks, block_step, 0)

    lane = lax.broadcasted_iota(jnp.int32, (1, 128), 1)
    for z in range(n_st):
        log_row = pltpu.roll(sums[0:1, :], 128 - z * group, 1) if z else sums[0:1, :]
        sim_row = pltpu.roll(sums[1:2, :], (128 + group - z * group) % 128, 1) if z != 1 else sums[1:2, :]
        tell[z, 0:1, :] = jnp.where(lane < group, log_row, sim_row)

    def tell_copy(offset, slot):
        to_ev, to_st = peer(offset)
        return pltpu.make_async_remote_copy(
            src_ref=tell.at[to_st, pl.ds(0, 1), :],
            dst_ref=heard.at[slot, pl.ds(0, 1), :],
            send_sem=tell_send.at[offset],
            recv_sem=tell_recv.at[slot],
            device_id=(to_ev, to_st),
            device_id_type=MESH,
        )

    for offset in range(1, n_dev):
        tell_copy(offset, me).start()
    heard[me, 0:1, :] = tell[st, 0:1, :]

    for offset in range(1, n_dev):
        count_copy(offset, lax.rem(me + offset, n_dev)).wait_recv()
    n_data = count_heard[0, 0:1, :]
    for index in range(1, n_dev):
        n_data = n_data + count_heard[index, 0:1, :]
    n_sim = events - n_data
    ratio = jnp.broadcast_to((n_sim / n_data)[:, 0:1], (2 * starts, BLOCK))
    final = jnp.broadcast_to((waves * scale / n_sim)[:, 0:1], (8, width))

    def scale_step(step, carry):
        first = step * BLOCK
        is_data = first + lax.broadcasted_iota(jnp.int32, (2 * starts, BLOCK), 1) < limit
        w = raw[step]
        here = pl.ds(pl.multiple_of(first, BLOCK), BLOCK)
        weights[:, here] = jnp.where(is_data, w * ratio, w).astype(BF16)
        return carry

    lax.fori_loop(0, blocks, scale_step, 0)

    def place(index):
        return 8 * (index // per), width * (index % per)

    def core_copy(part):
        return pltpu.make_async_remote_copy(
            src_ref=mine.at[part, 1 - core],
            dst_ref=core_in.at[part],
            send_sem=core_send.at[part],
            recv_sem=core_recv.at[part],
            device_id=(2 * plane + 1 - core, st),
            device_id_type=MESH,
        )

    def plane_copy(part, offset):
        to = lax.rem(plane + offset, planes)
        return pltpu.make_async_remote_copy(
            src_ref=plane_sum.at[part, to],
            dst_ref=plane_in.at[part, offset],
            send_sem=plane_send.at[part, offset],
            recv_sem=plane_recv.at[part, offset],
            device_id=(2 * to + core, st),
            device_id_type=MESH,
        )

    def st_copy(part, offset):
        to = lax.rem(st + offset, n_st)
        return pltpu.make_async_remote_copy(
            src_ref=st_sum.at[part, to],
            dst_ref=st_in.at[part, offset],
            send_sem=st_send.at[part, offset],
            recv_sem=st_recv.at[part, offset],
            device_id=(ev, to),
            device_id_type=MESH,
        )

    def done_copy(part, offset, slot):
        return pltpu.make_async_remote_copy(
            src_ref=done.at[part],
            dst_ref=done_in.at[part, slot],
            send_sem=done_send.at[part, offset],
            recv_sem=done_recv.at[part, slot],
            device_id=(lax.rem(ev + offset, n_ev), st),
            device_id_type=MESH,
        )

    slot = core * planes + plane

    def make_part(part):
        real_cols = pl.ds(part * part_waves, part_waves)
        imag_cols = pl.ds(waves + part * part_waves, part_waves)
        by_real = jnp.dot(weights[...], amp_ref[:, real_cols], preferred_element_type=F32)
        by_imag = jnp.dot(weights[...], amp_ref[:, imag_cols], preferred_element_type=F32)
        grad = jnp.concatenate(
            [by_real[:starts] + by_imag[starts:], by_real[starts:] - by_imag[:starts]], 1
        )
        for c in range(2):
            for p in range(planes):
                row, col = place(c * planes + p)
                for z in range(n_st):
                    at = z * group + row
                    mine[part, c, p, z] = grad[at : at + 8, col : col + width] * final
        core_copy(part).start()

    def plane_stage(part):
        core_copy(part).wait_recv()
        plane_sum[part] = mine[part, core] + core_in[part]
        for offset in range(1, planes):
            plane_copy(part, offset).start()

    def st_stage(part):
        total = plane_sum[part, plane]
        for offset in range(1, planes):
            plane_copy(part, offset).wait_recv()
            total = total + plane_in[part, offset]
        st_sum[part] = total
        for offset in range(1, n_st):
            st_copy(part, offset).start()

    def done_stage(part):
        total = st_sum[part, st]
        for offset in range(1, n_st):
            st_copy(part, offset).wait_recv()
            total = total + st_in[part, offset]
        done[part] = total
        for offset in range(1, n_ev):
            done_copy(part, offset, slot).start()
        done_in[part, slot] = total

    for tick in range(parts + 3):
        if tick < parts:
            make_part(tick)
        if 0 <= tick - 3 < parts:
            done_stage(tick - 3)
        if 0 <= tick - 2 < parts:
            st_stage(tick - 2)
        if 0 <= tick - 1 < parts:
            plane_stage(tick - 1)

    for offset in range(1, n_dev):
        tell_copy(offset, lax.rem(me + offset, n_dev)).wait_recv()
    total = heard[0, 0:1, :]
    for index in range(1, n_dev):
        total = total + heard[index, 0:1, :]
    like_ref[...] = pltpu.roll(total, 128 - group, 1) / n_sim - total / n_data

    for part in range(parts):
        for offset in range(1, n_ev):
            other = lax.rem(ev + offset, n_ev)
            done_copy(part, offset, lax.rem(other, 2) * planes + other // 2).wait_recv()
        for index in range(n_ev):
            row, col = place(index)
            at = part * part_waves + col
            if col >= part_waves:
                at += waves - part_waves
            out_ref[row : row + 8, at : at + width] = done_in[part, index]

    for offset in range(1, n_dev):
        count_copy(offset, me).wait_send()
        tell_copy(offset, me).wait_send()
    for part in range(parts):
        core_copy(part).wait_send()
        for offset in range(1, planes):
            plane_copy(part, offset).wait_send()
        for offset in range(1, n_st):
            st_copy(part, offset).wait_send()
        for offset in range(1, n_ev):
            done_copy(part, offset, slot).wait_send()


def solution(mesh):
    n_ev = mesh.shape["ev"]
    n_st = mesh.shape["st"]
    n_dev = n_ev * n_st
    planes = n_ev // 2
    dma = pltpu.SemaphoreType.DMA
    vmem = pltpu.VMEM
    smem = pltpu.SMEM

    def shards(
        amplitudes, event_mass, data_rows, wave_shape, pole_mass, pole_width, coefficients, background
    ):
        rows, wide = amplitudes.shape
        waves = wide // 2
        starts = coefficients.shape[0]
        shapes = pole_mass.shape[0]
        group = starts // n_st
        parts = 4
        while (group // 8) * (wide // parts // 128) % n_ev:
            parts //= 2
        width = group * wide // (8 * n_ev * parts)
        blocks = rows // BLOCK
        piece = (8, width)
        gradient, like = pl.pallas_call(
            functools.partial(fit_kernel, n_ev, n_st, parts),
            in_specs=[pl.BlockSpec(memory_space=pltpu.HBM)] * 8,
            out_specs=[pl.BlockSpec(memory_space=pltpu.VMEM)] * 2,
            out_shape=[
                jax.ShapeDtypeStruct((group, wide), F32),
                jax.ShapeDtypeStruct((1, 128), F32),
            ],
            scratch_shapes=[
                smem((1,), jnp.int32),
                smem((shapes,), F32),
                smem((shapes,), F32),
                vmem((rows, wide), BF16),
                vmem((blocks, 1, BLOCK), F32),
                vmem((1, waves), jnp.int32),
                vmem((starts, wide), F32),
                vmem((1, starts), F32),
                vmem((wide, 2 * starts), BF16),
                vmem((8, waves), F32),
                vmem((8, waves), F32),
                vmem((BLOCK, 128), F32),
                vmem((8, 128), F32),
                vmem((blocks, 2 * starts, BLOCK), F32),
                vmem((2 * starts, rows), BF16),
                vmem((8, 128), F32),
                vmem((n_dev, 8, 128), F32),
                vmem((n_st, 8, 128), F32),
                vmem((n_dev, 8, 128), F32),
                vmem((parts, 2, planes, n_st, *piece), F32),
                vmem((parts, planes, n_st, *piece), F32),
                vmem((parts, planes, n_st, *piece), F32),
                vmem((parts, planes, n_st, *piece), F32),
                vmem((parts, n_st, *piece), F32),
                vmem((parts, n_st, *piece), F32),
                vmem((parts, *piece), F32),
                vmem((parts, n_ev, *piece), F32),
                dma((7,)),
                dma((blocks,)),
                dma((n_dev,)),
                dma((n_dev,)),
                dma((n_dev,)),
                dma((n_dev,)),
                dma((parts,)),
                dma((parts,)),
                dma((parts, planes)),
                dma((parts, planes)),
                dma((parts, n_st)),
                dma((parts, n_st)),
                dma((parts, n_ev)),
                dma((parts, n_ev)),
            ],
            compiler_params=pltpu.CompilerParams(
                collective_id=0, has_side_effects=True, vmem_limit_bytes=56 * 1024 * 1024
            ),
            name="fit_all",
        )(
            data_rows,
            pole_mass,
            pole_width,
            amplitudes,
            event_mass.reshape(blocks, 1, BLOCK),
            wave_shape.reshape(1, waves),
            coefficients,
            background.reshape(1, starts),
        )
        return gradient, like[0, :group]

    return jax.shard_map(
        shards,
        mesh=mesh,
        in_specs=(P(("ev", "st"), None), P(("ev", "st")), P(("ev", "st")), P(), P(), P(), P(), P()),
        out_specs=(P("st", None), P("st")),
        check_vma=False,
    )
```

```python
import functools

import jax
import jax.numpy as jnp
from jax import lax
from jax.experimental import pallas as pl
from jax.experimental.pallas import tpu as pltpu
from jax.sharding import PartitionSpec as P

BLOCK = 512
ROWS = 16
LANES = 256
MESH = pl.DeviceIdType.MESH
F32 = jnp.float32
BF16 = jnp.bfloat16


def fit_kernel(
    n_ev,
    n_st,
    parts,
    limit_hbm,
    pole_mass_hbm,
    pole_width_hbm,
    amp_hbm,
    mass_hbm,
    wave_hbm,
    coef_hbm,
    back_hbm,
    out_ref,
    like_ref,
    limit_ref,
    pole_mass_ref,
    pole_width_ref,
    amp_ref,
    mass_ref,
    wave_ref,
    coef_ref,
    back_ref,
    mix,
    square,
    inverse,
    mass2,
    sums,
    raw,
    weights,
    tiny,
    tiny_core,
    tiny_plane,
    tiny_st,
    mine,
    core_in,
    plane_sum,
    plane_in,
    st_sum,
    st_in,
    done,
    done_in,
    load_sem,
    amp_sem,
    tiny_send,
    tiny_recv,
    core_send,
    core_recv,
    plane_send,
    plane_recv,
    st_send,
    st_recv,
    done_send,
    done_recv,
):
    ev = lax.axis_index("ev")
    st = lax.axis_index("st")
    n_dev = n_ev * n_st
    planes = n_ev // 2
    core = lax.rem(ev, 2)
    plane = lax.div(ev, 2)
    rows, wide = amp_ref.shape
    waves = wide // 2
    starts = back_ref.shape[1]
    group = starts // n_st
    events = rows * n_dev
    blocks = rows // BLOCK
    scale = waves ** (-0.5)
    width = mine.shape[-1]
    part_waves = waves // parts
    per = 2 * part_waves // width

    partner = (ev + 1 - 2 * core, st)
    plane_at = [lax.rem(plane + offset, planes) for offset in range(planes)]
    plane_to = [(2 * at + core, st) for at in plane_at]
    st_at = [lax.rem(st + offset, n_st) for offset in range(n_st)]
    ev_at = [lax.rem(ev + offset, n_ev) for offset in range(n_ev)]

    barrier = pltpu.get_barrier_semaphore()
    for offset in range(1, n_ev):
        pl.semaphore_signal(barrier, inc=1, device_id=(ev_at[offset], st), device_id_type=MESH)
    for offset in range(1, n_st):
        pl.semaphore_signal(barrier, inc=1, device_id=(ev, st_at[offset]), device_id_type=MESH)

    loads = [
        pltpu.make_async_copy(src, dst, load_sem.at[index])
        for index, (src, dst) in enumerate(
            [
                (coef_hbm, coef_ref),
                (wave_hbm, wave_ref),
                (limit_hbm, limit_ref),
                (pole_mass_hbm, pole_mass_ref),
                (pole_width_hbm, pole_width_ref),
                (mass_hbm, mass_ref),
                (back_hbm, back_ref),
            ]
        )
    ]
    for load in loads:
        load.start()

    def fetch(index):
        here = pl.ds(pl.multiple_of(index * BLOCK, BLOCK), BLOCK)
        return pltpu.make_async_copy(amp_hbm.at[here, :], amp_ref.at[here, :], amp_sem.at[index])

    for index in range(blocks):
        fetch(index).start()

    for load in loads:
        load.wait()
    limit = limit_ref[0]
    which = wave_ref[...]
    peak = jnp.zeros(which.shape, F32)
    center = jnp.zeros(which.shape, F32)
    for k in range(pole_mass_ref.shape[0]):
        mass_k = pole_mass_ref[k]
        peak = jnp.where(which == k, mass_k * pole_width_ref[k], peak)
        center = jnp.where(which == k, mass_k * mass_k, center)
    square[...] = jnp.broadcast_to(center, square.shape)
    inverse[...] = jnp.broadcast_to(1.0 / peak, inverse.shape)
    coef_real = coef_ref[:, :waves].T
    coef_imag = coef_ref[:, waves:].T
    mix[:waves, :starts] = coef_real.astype(BF16)
    mix[:waves, starts:] = coef_imag.astype(BF16)
    mix[waves:, :starts] = (-coef_imag).astype(BF16)
    mix[waves:, starts:] = coef_real.astype(BF16)
    sums[...] = jnp.zeros_like(sums)

    def tiny_copy(kind, stage, dst, send, recv, to):
        return pltpu.make_async_remote_copy(
            src_ref=tiny.at[kind, stage],
            dst_ref=dst,
            send_sem=tiny_send.at[kind, send],
            recv_sem=tiny_recv.at[kind, recv],
            device_id=to,
            device_id_type=MESH,
        )

    def tiny_core_copy(kind):
        return tiny_copy(kind, 0, tiny_core.at[kind], 0, 0, partner)

    def tiny_plane_copy(kind, offset, at):
        return tiny_copy(kind, 1, tiny_plane.at[kind, at], offset, 1 + at, plane_to[offset])

    def tiny_st_copy(kind, offset, at):
        return tiny_copy(
            kind,
            2,
            tiny_st.at[kind, at],
            planes + offset,
            1 + planes + at,
            (ev, st_at[offset]),
        )

    def tiny_core_stage(kind, value):
        tiny[kind, 0] = value
        tiny_core_copy(kind).start()

    def tiny_plane_stage(kind):
        tiny_core_copy(kind).wait_recv()
        value = tiny[kind, 0] + tiny_core[kind]
        tiny[kind, 1] = value
        for offset in range(1, planes):
            tiny_plane_copy(kind, offset, plane).start()
        tiny_plane[kind, plane] = value

    def tiny_st_stage(kind):
        for offset in range(1, planes):
            tiny_plane_copy(kind, offset, plane_at[offset]).wait_recv()
        value = tiny_plane[kind, 0]
        for index in range(1, planes):
            value = value + tiny_plane[kind, index]
        tiny[kind, 2] = value
        for offset in range(1, n_st):
            tiny_st_copy(kind, offset, st).start()
        tiny_st[kind, st] = value

    def tiny_total(kind):
        for offset in range(1, n_st):
            tiny_st_copy(kind, offset, st_at[offset]).wait_recv()
        value = tiny_st[kind, 0]
        for index in range(1, n_st):
            value = value + tiny_st[kind, index]
        return value

    def block_step(step, carry):
        first = pl.multiple_of(step * BLOCK, BLOCK)
        fetch(step).wait()

        @pl.when(step == 1)
        def _():
            pl.semaphore_wait(barrier, n_ev + n_st - 2)
            tiny_core_stage(0, jnp.full((8, 128), limit, jnp.int32).astype(F32))

        @pl.when(step == 2)
        def _():
            tiny_plane_stage(0)

        @pl.when(step == 3)
        def _():
            tiny_st_stage(0)

        mass = mass_ref[step]
        mass2[...] = jnp.broadcast_to(mass * mass, (128, BLOCK)).T

        def dress(index, carry):
            row = pl.multiple_of(index * ROWS, ROWS)
            here = pl.ds(pl.multiple_of(first + row, ROWS), ROWS)
            m2 = mass2[pl.ds(row, ROWS), :]
            m2 = jnp.concatenate([m2] * (LANES // 128), 1)
            for col in range(0, waves, LANES):
                real_cols = pl.ds(col, LANES)
                imag_cols = pl.ds(waves + col, LANES)
                sq = jnp.concatenate([square[:, real_cols]] * (ROWS // 8), 0)
                inv = jnp.concatenate([inverse[:, real_cols]] * (ROWS // 8), 0)
                u = (sq - m2) * inv
                denom = u * u + 1.0
                guess = pl.reciprocal(denom, approx=True)
                r = guess * (2.0 - denom * guess)
                amp_real = amp_ref[here, real_cols].astype(F32)
                amp_imag = amp_ref[here, imag_cols].astype(F32)
                amp_ref[here, real_cols] = ((amp_real * u - amp_imag) * r).astype(BF16)
                amp_ref[here, imag_cols] = ((amp_imag * u + amp_real) * r).astype(BF16)
            return carry

        lax.fori_loop(0, BLOCK // ROWS, dress, 0)

        dressed = amp_ref[pl.ds(first, BLOCK), :]
        value = jnp.dot(dressed, mix[...], preferred_element_type=F32) * scale
        val_real = value[:, :starts]
        val_imag = value[:, starts:]
        intensity = val_real * val_real + val_imag * val_imag + back_ref[...]
        is_data = first + lax.broadcasted_iota(jnp.int32, (BLOCK, starts), 0) < limit
        sums[0:1, :] += jnp.sum(jnp.where(is_data, jnp.log(intensity), 0.0), 0, keepdims=True)
        sums[1:2, :] += jnp.sum(jnp.where(is_data, 0.0, intensity), 0, keepdims=True)
        factor = jnp.where(is_data, -2.0 / intensity, 2.0)
        raw[step] = jnp.concatenate([factor * val_real, factor * val_imag], 1).T
        return carry

    lax.fori_loop(0, blocks, block_step, 0)

    tiny_core_stage(1, sums[...])
    n_data = tiny_total(0)[0:1, :]
    n_sim = events - n_data
    ratio = jnp.broadcast_to((n_sim / n_data)[:, 0:1], (2 * starts, BLOCK))
    final = jnp.broadcast_to((waves * scale / n_sim)[:, 0:1], (8, width))

    def scale_step(step, carry):
        first = step * BLOCK
        is_data = first + lax.broadcasted_iota(jnp.int32, (2 * starts, BLOCK), 1) < limit
        w = raw[step]
        here = pl.ds(pl.multiple_of(first, BLOCK), BLOCK)
        weights[:, here] = jnp.where(is_data, w * ratio, w).astype(BF16)
        return carry

    lax.fori_loop(0, blocks, scale_step, 0)

    def place(index):
        return 8 * (index // per), width * (index % per)

    def core_copy(part):
        return pltpu.make_async_remote_copy(
            src_ref=mine.at[part, 1 - core],
            dst_ref=core_in.at[part],
            send_sem=core_send.at[part],
            recv_sem=core_recv.at[part],
            device_id=partner,
            device_id_type=MESH,
        )

    def plane_copy(part, offset):
        to = plane_at[offset]
        return pltpu.make_async_remote_copy(
            src_ref=plane_sum.at[part, to],
            dst_ref=plane_in.at[part, offset],
            send_sem=plane_send.at[part, offset],
            recv_sem=plane_recv.at[part, offset],
            device_id=plane_to[offset],
            device_id_type=MESH,
        )

    def st_copy(part, offset):
        to = st_at[offset]
        return pltpu.make_async_remote_copy(
            src_ref=st_sum.at[part, to],
            dst_ref=st_in.at[part, offset],
            send_sem=st_send.at[part, offset],
            recv_sem=st_recv.at[part, offset],
            device_id=(ev, to),
            device_id_type=MESH,
        )

    def done_copy(part, offset, slot):
        return pltpu.make_async_remote_copy(
            src_ref=done.at[part],
            dst_ref=done_in.at[part, slot],
            send_sem=done_send.at[part, offset],
            recv_sem=done_recv.at[part, slot],
            device_id=(ev_at[offset], st),
            device_id_type=MESH,
        )

    slot = core * planes + plane
    ev_slot = [lax.rem(at, 2) * planes + lax.div(at, 2) for at in ev_at]

    def make_part(part):
        real_cols = pl.ds(part * part_waves, part_waves)
        imag_cols = pl.ds(waves + part * part_waves, part_waves)
        by_real = jnp.dot(weights[...], amp_ref[:, real_cols], preferred_element_type=F32)
        by_imag = jnp.dot(weights[...], amp_ref[:, imag_cols], preferred_element_type=F32)
        grad = jnp.concatenate(
            [by_real[:starts] + by_imag[starts:], by_real[starts:] - by_imag[:starts]], 1
        )
        for c in range(2):
            for p in range(planes):
                row, col = place(c * planes + p)
                for z in range(n_st):
                    at = z * group + row
                    mine[part, c, p, z] = grad[at : at + 8, col : col + width] * final
        core_copy(part).start()

    def plane_stage(part):
        core_copy(part).wait_recv()
        plane_sum[part] = mine[part, core] + core_in[part]
        for offset in range(1, planes):
            plane_copy(part, offset).start()

    def st_stage(part):
        total = plane_sum[part, plane]
        for offset in range(1, planes):
            plane_copy(part, offset).wait_recv()
            total = total + plane_in[part, offset]
        st_sum[part] = total
        for offset in range(1, n_st):
            st_copy(part, offset).start()

    def done_stage(part):
        total = st_sum[part, st]
        for offset in range(1, n_st):
            st_copy(part, offset).wait_recv()
            total = total + st_in[part, offset]
        done[part] = total
        for offset in range(1, n_ev):
            done_copy(part, offset, slot).start()
        done_in[part, slot] = total

    for tick in range(parts + 3):
        if tick < parts:
            make_part(tick)
        if 0 <= tick - 3 < parts:
            done_stage(tick - 3)
        if 0 <= tick - 2 < parts:
            st_stage(tick - 2)
        if 0 <= tick - 1 < parts:
            plane_stage(tick - 1)
        if tick == 0:
            tiny_plane_stage(1)
        if tick == 1:
            tiny_st_stage(1)

    total = tiny_total(1)
    like_all = total[1:2, :] / n_sim - total[0:1, :] / n_data
    like = like_all
    for z in range(1, n_st):
        like = jnp.where(st == z, pltpu.roll(like_all, 128 - z * group, 1), like)
    like_ref[...] = like

    for part in range(parts):
        for offset in range(1, n_ev):
            done_copy(part, offset, ev_slot[offset]).wait_recv()
        for index in range(n_ev):
            row, col = place(index)
            at = part * part_waves + col
            if col >= part_waves:
                at += waves - part_waves
            out_ref[row : row + 8, at : at + width] = done_in[part, index]

    for kind in range(2):
        tiny_core_copy(kind).wait_send()
        for offset in range(1, planes):
            tiny_plane_copy(kind, offset, plane).wait_send()
        for offset in range(1, n_st):
            tiny_st_copy(kind, offset, st).wait_send()
    for part in range(parts):
        core_copy(part).wait_send()
        for offset in range(1, planes):
            plane_copy(part, offset).wait_send()
        for offset in range(1, n_st):
            st_copy(part, offset).wait_send()
        for offset in range(1, n_ev):
            done_copy(part, offset, slot).wait_send()


def solution(mesh):
    n_ev = mesh.shape["ev"]
    n_st = mesh.shape["st"]
    n_dev = n_ev * n_st
    planes = n_ev // 2
    dma = pltpu.SemaphoreType.DMA
    vmem = pltpu.VMEM
    smem = pltpu.SMEM

    def shards(
        amplitudes, event_mass, data_rows, wave_shape, pole_mass, pole_width, coefficients, background
    ):
        rows, wide = amplitudes.shape
        waves = wide // 2
        starts = coefficients.shape[0]
        shapes = pole_mass.shape[0]
        group = starts // n_st
        parts = 4
        while (group // 8) * (wide // parts // 128) % n_ev:
            parts //= 2
        width = group * wide // (8 * n_ev * parts)
        blocks = rows // BLOCK
        piece = (8, width)
        gradient, like = pl.pallas_call(
            functools.partial(fit_kernel, n_ev, n_st, parts),
            in_specs=[pl.BlockSpec(memory_space=pltpu.HBM)] * 8,
            out_specs=[pl.BlockSpec(memory_space=pltpu.VMEM)] * 2,
            out_shape=[
                jax.ShapeDtypeStruct((group, wide), F32),
                jax.ShapeDtypeStruct((1, 128), F32),
            ],
            scratch_shapes=[
                smem((1,), jnp.int32),
                smem((shapes,), F32),
                smem((shapes,), F32),
                vmem((rows, wide), BF16),
                vmem((blocks, 1, BLOCK), F32),
                vmem((1, waves), jnp.int32),
                vmem((starts, wide), F32),
                vmem((1, starts), F32),
                vmem((wide, 2 * starts), BF16),
                vmem((8, waves), F32),
                vmem((8, waves), F32),
                vmem((BLOCK, 128), F32),
                vmem((8, 128), F32),
                vmem((blocks, 2 * starts, BLOCK), F32),
                vmem((2 * starts, rows), BF16),
                vmem((2, 3, 8, 128), F32),
                vmem((2, 8, 128), F32),
                vmem((2, planes, 8, 128), F32),
                vmem((2, n_st, 8, 128), F32),
                vmem((parts, 2, planes, n_st, *piece), F32),
                vmem((parts, planes, n_st, *piece), F32),
                vmem((parts, planes, n_st, *piece), F32),
                vmem((parts, planes, n_st, *piece), F32),
                vmem((parts, n_st, *piece), F32),
                vmem((parts, n_st, *piece), F32),
                vmem((parts, *piece), F32),
                vmem((parts, n_ev, *piece), F32),
                dma((7,)),
                dma((blocks,)),
                dma((2, planes + n_st)),
                dma((2, 1 + planes + n_st)),
                dma((parts,)),
                dma((parts,)),
                dma((parts, planes)),
                dma((parts, planes)),
                dma((parts, n_st)),
                dma((parts, n_st)),
                dma((parts, n_ev)),
                dma((parts, n_ev)),
            ],
            compiler_params=pltpu.CompilerParams(
                collective_id=0, has_side_effects=True, vmem_limit_bytes=56 * 1024 * 1024
            ),
            name="fit_all",
        )(
            data_rows,
            pole_mass,
            pole_width,
            amplitudes,
            event_mass.reshape(blocks, 1, BLOCK),
            wave_shape.reshape(1, waves),
            coefficients,
            background.reshape(1, starts),
        )
        return gradient, like[0, :group]

    return jax.shard_map(
        shards,
        mesh=mesh,
        in_specs=(P(("ev", "st"), None), P(("ev", "st")), P(("ev", "st")), P(), P(), P(), P(), P()),
        out_specs=(P("st", None), P("st")),
        check_vma=False,
    )
```

```python
import functools

import jax
import jax.numpy as jnp
from jax import lax
from jax.experimental import pallas as pl
from jax.experimental.pallas import tpu as pltpu
from jax.sharding import PartitionSpec as P

BLOCK = 512
ROWS = 16
LANES = 256
MESH = pl.DeviceIdType.MESH
F32 = jnp.float32
BF16 = jnp.bfloat16


def fit_kernel(
    n_ev,
    n_st,
    parts,
    limit_hbm,
    pole_mass_hbm,
    pole_width_hbm,
    amp_hbm,
    mass_hbm,
    wave_hbm,
    coef_hbm,
    back_hbm,
    out_ref,
    like_ref,
    limit_ref,
    pole_mass_ref,
    pole_width_ref,
    amp_ref,
    mass_ref,
    wave_ref,
    coef_ref,
    back_ref,
    mix,
    square,
    inverse,
    mass2,
    sums,
    raw,
    weights,
    tiny,
    tiny_core,
    tiny_plane,
    tiny_st,
    mine,
    core_in,
    plane_sum,
    plane_in,
    st_sum,
    st_in,
    done,
    done_in,
    load_sem,
    amp_sem,
    tiny_send,
    tiny_recv,
    core_send,
    core_recv,
    plane_send,
    plane_recv,
    st_send,
    st_recv,
    done_send,
    done_recv,
):
    ev = lax.axis_index("ev")
    st = lax.axis_index("st")
    n_dev = n_ev * n_st
    planes = n_ev // 2
    core = lax.rem(ev, 2)
    plane = lax.div(ev, 2)
    rows, wide = amp_ref.shape
    waves = wide // 2
    starts = back_ref.shape[1]
    group = starts // n_st
    events = rows * n_dev
    blocks = rows // BLOCK
    scale = waves ** (-0.5)
    width = mine.shape[-1]
    part_waves = waves // parts
    per = 2 * part_waves // width

    partner = (ev + 1 - 2 * core, st)
    plane_at = [lax.rem(plane + offset, planes) for offset in range(planes)]
    plane_to = [(2 * at + core, st) for at in plane_at]
    st_at = [lax.rem(st + offset, n_st) for offset in range(n_st)]
    ev_at = [lax.rem(ev + offset, n_ev) for offset in range(n_ev)]

    barrier = pltpu.get_barrier_semaphore()
    for offset in range(1, n_ev):
        pl.semaphore_signal(barrier, inc=1, device_id=(ev_at[offset], st), device_id_type=MESH)
    for offset in range(1, n_st):
        pl.semaphore_signal(barrier, inc=1, device_id=(ev, st_at[offset]), device_id_type=MESH)

    loads = [
        pltpu.make_async_copy(src, dst, load_sem.at[index])
        for index, (src, dst) in enumerate(
            [
                (coef_hbm, coef_ref),
                (wave_hbm, wave_ref),
                (limit_hbm, limit_ref),
                (pole_mass_hbm, pole_mass_ref),
                (pole_width_hbm, pole_width_ref),
                (mass_hbm, mass_ref),
                (back_hbm, back_ref),
            ]
        )
    ]
    for load in loads:
        load.start()

    def fetch(index):
        here = pl.ds(pl.multiple_of(index * BLOCK, BLOCK), BLOCK)
        return pltpu.make_async_copy(amp_hbm.at[here, :], amp_ref.at[here, :], amp_sem.at[index])

    for index in range(blocks):
        fetch(index).start()

    for load in loads:
        load.wait()
    limit = limit_ref[0]
    which = wave_ref[...]
    peak = jnp.zeros(which.shape, F32)
    center = jnp.zeros(which.shape, F32)
    for k in range(pole_mass_ref.shape[0]):
        mass_k = pole_mass_ref[k]
        peak = jnp.where(which == k, mass_k * pole_width_ref[k], peak)
        center = jnp.where(which == k, mass_k * mass_k, center)
    square[...] = jnp.broadcast_to(center, square.shape)
    inverse[...] = jnp.broadcast_to(1.0 / peak, inverse.shape)
    coef_real = coef_ref[:, :waves].T
    coef_imag = coef_ref[:, waves:].T
    mix[:waves, :starts] = coef_real.astype(BF16)
    mix[:waves, starts:] = coef_imag.astype(BF16)
    mix[waves:, :starts] = (-coef_imag).astype(BF16)
    mix[waves:, starts:] = coef_real.astype(BF16)
    sums[...] = jnp.zeros_like(sums)

    def tiny_copy(kind, stage, dst, send, recv, to):
        return pltpu.make_async_remote_copy(
            src_ref=tiny.at[kind, stage],
            dst_ref=dst,
            send_sem=tiny_send.at[kind, send],
            recv_sem=tiny_recv.at[kind, recv],
            device_id=to,
            device_id_type=MESH,
        )

    def tiny_core_copy(kind):
        return tiny_copy(kind, 0, tiny_core.at[kind], 0, 0, partner)

    def tiny_plane_copy(kind, offset, at):
        return tiny_copy(kind, 1, tiny_plane.at[kind, at], offset, 1 + at, plane_to[offset])

    def tiny_st_copy(kind, offset, at):
        return tiny_copy(
            kind,
            2,
            tiny_st.at[kind, at],
            planes + offset,
            1 + planes + at,
            (ev, st_at[offset]),
        )

    def tiny_core_stage(kind, value):
        tiny[kind, 0] = value
        tiny_core_copy(kind).start()

    def tiny_plane_stage(kind):
        tiny_core_copy(kind).wait_recv()
        value = tiny[kind, 0] + tiny_core[kind]
        tiny[kind, 1] = value
        for offset in range(1, planes):
            tiny_plane_copy(kind, offset, plane).start()
        tiny_plane[kind, plane] = value

    def tiny_st_stage(kind):
        for offset in range(1, planes):
            tiny_plane_copy(kind, offset, plane_at[offset]).wait_recv()
        value = tiny_plane[kind, 0]
        for index in range(1, planes):
            value = value + tiny_plane[kind, index]
        tiny[kind, 2] = value
        for offset in range(1, n_st):
            tiny_st_copy(kind, offset, st).start()
        tiny_st[kind, st] = value

    def tiny_total(kind):
        for offset in range(1, n_st):
            tiny_st_copy(kind, offset, st_at[offset]).wait_recv()
        value = tiny_st[kind, 0]
        for index in range(1, n_st):
            value = value + tiny_st[kind, index]
        return value

    def block_step(step, carry):
        first = pl.multiple_of(step * BLOCK, BLOCK)
        fetch(step).wait()

        @pl.when(step == 1)
        def _():
            pl.semaphore_wait(barrier, n_ev + n_st - 2)
            tiny_core_stage(0, jnp.full((8, 128), limit, jnp.int32).astype(F32))

        @pl.when(step == 2)
        def _():
            tiny_plane_stage(0)

        @pl.when(step == 3)
        def _():
            tiny_st_stage(0)

        mass = mass_ref[step]
        mass2[...] = jnp.broadcast_to(mass * mass, (128, BLOCK)).T

        def dress(index, carry):
            row = pl.multiple_of(index * ROWS, ROWS)
            here = pl.ds(pl.multiple_of(first + row, ROWS), ROWS)
            m2 = mass2[pl.ds(row, ROWS), :]
            m2 = jnp.concatenate([m2] * (LANES // 128), 1)
            for col in range(0, waves, LANES):
                real_cols = pl.ds(col, LANES)
                imag_cols = pl.ds(waves + col, LANES)
                sq = jnp.concatenate([square[:, real_cols]] * (ROWS // 8), 0)
                inv = jnp.concatenate([inverse[:, real_cols]] * (ROWS // 8), 0)
                u = (sq - m2) * inv
                denom = u * u + 1.0
                guess = pl.reciprocal(denom, approx=True)
                r = guess * (2.0 - denom * guess)
                amp_real = amp_ref[here, real_cols].astype(F32)
                amp_imag = amp_ref[here, imag_cols].astype(F32)
                amp_ref[here, real_cols] = ((amp_real * u - amp_imag) * r).astype(BF16)
                amp_ref[here, imag_cols] = ((amp_imag * u + amp_real) * r).astype(BF16)
            return carry

        lax.fori_loop(0, BLOCK // ROWS, dress, 0, unroll=2)

        dressed = amp_ref[pl.ds(first, BLOCK), :]
        value = jnp.dot(dressed, mix[...], preferred_element_type=F32) * scale
        val_real = value[:, :starts]
        val_imag = value[:, starts:]
        intensity = val_real * val_real + val_imag * val_imag + back_ref[...]
        is_data = first + lax.broadcasted_iota(jnp.int32, (BLOCK, starts), 0) < limit
        sums[0:1, :] += jnp.sum(jnp.where(is_data, jnp.log(intensity), 0.0), 0, keepdims=True)
        sums[1:2, :] += jnp.sum(jnp.where(is_data, 0.0, intensity), 0, keepdims=True)
        factor = jnp.where(is_data, -2.0 / intensity, 2.0)
        raw[step] = jnp.concatenate([factor * val_real, factor * val_imag], 1).T
        return carry

    lax.fori_loop(0, blocks, block_step, 0)

    tiny_core_stage(1, sums[...])
    n_data = tiny_total(0)[0:1, :]
    n_sim = events - n_data
    ratio = jnp.broadcast_to((n_sim / n_data)[:, 0:1], (2 * starts, BLOCK))
    final = jnp.broadcast_to((waves * scale / n_sim)[:, 0:1], (8, width))

    def scale_step(step, carry):
        first = step * BLOCK
        is_data = first + lax.broadcasted_iota(jnp.int32, (2 * starts, BLOCK), 1) < limit
        w = raw[step]
        here = pl.ds(pl.multiple_of(first, BLOCK), BLOCK)
        weights[:, here] = jnp.where(is_data, w * ratio, w).astype(BF16)
        return carry

    lax.fori_loop(0, blocks, scale_step, 0)

    def place(index):
        return 8 * (index // per), width * (index % per)

    def core_copy(part):
        return pltpu.make_async_remote_copy(
            src_ref=mine.at[part, 1 - core],
            dst_ref=core_in.at[part],
            send_sem=core_send.at[part],
            recv_sem=core_recv.at[part],
            device_id=partner,
            device_id_type=MESH,
        )

    def plane_copy(part, offset):
        to = plane_at[offset]
        return pltpu.make_async_remote_copy(
            src_ref=plane_sum.at[part, to],
            dst_ref=plane_in.at[part, offset],
            send_sem=plane_send.at[part, offset],
            recv_sem=plane_recv.at[part, offset],
            device_id=plane_to[offset],
            device_id_type=MESH,
        )

    def st_copy(part, offset):
        to = st_at[offset]
        return pltpu.make_async_remote_copy(
            src_ref=st_sum.at[part, to],
            dst_ref=st_in.at[part, offset],
            send_sem=st_send.at[part, offset],
            recv_sem=st_recv.at[part, offset],
            device_id=(ev, to),
            device_id_type=MESH,
        )

    def done_copy(part, offset, slot):
        return pltpu.make_async_remote_copy(
            src_ref=done.at[part],
            dst_ref=done_in.at[part, slot],
            send_sem=done_send.at[part, offset],
            recv_sem=done_recv.at[part, slot],
            device_id=(ev_at[offset], st),
            device_id_type=MESH,
        )

    slot = core * planes + plane
    ev_slot = [lax.rem(at, 2) * planes + lax.div(at, 2) for at in ev_at]

    def make_part(part):
        real_cols = pl.ds(part * part_waves, part_waves)
        imag_cols = pl.ds(waves + part * part_waves, part_waves)
        by_real = jnp.dot(weights[...], amp_ref[:, real_cols], preferred_element_type=F32)
        by_imag = jnp.dot(weights[...], amp_ref[:, imag_cols], preferred_element_type=F32)
        grad = jnp.concatenate(
            [by_real[:starts] + by_imag[starts:], by_real[starts:] - by_imag[:starts]], 1
        )
        for c in range(2):
            for p in range(planes):
                row, col = place(c * planes + p)
                for z in range(n_st):
                    at = z * group + row
                    mine[part, c, p, z] = grad[at : at + 8, col : col + width] * final
        core_copy(part).start()

    def plane_stage(part):
        core_copy(part).wait_recv()
        plane_sum[part] = mine[part, core] + core_in[part]
        for offset in range(1, planes):
            plane_copy(part, offset).start()

    def st_stage(part):
        total = plane_sum[part, plane]
        for offset in range(1, planes):
            plane_copy(part, offset).wait_recv()
            total = total + plane_in[part, offset]
        st_sum[part] = total
        for offset in range(1, n_st):
            st_copy(part, offset).start()

    def done_stage(part):
        total = st_sum[part, st]
        for offset in range(1, n_st):
            st_copy(part, offset).wait_recv()
            total = total + st_in[part, offset]
        done[part] = total
        for offset in range(1, n_ev):
            done_copy(part, offset, slot).start()
        done_in[part, slot] = total

    for part in range(parts):
        make_part(part)
        if part >= 1:
            plane_stage(part - 1)
        if part >= 3:
            st_stage(part - 3)
        if part == 0:
            tiny_plane_stage(1)
        if part == 1:
            tiny_st_stage(1)
    if parts >= 3:
        st_stage(parts - 3)
    plane_stage(parts - 1)
    for part in range(max(parts - 2, 0)):
        done_stage(part)
    if parts >= 2:
        st_stage(parts - 2)
    st_stage(parts - 1)
    for part in range(max(parts - 2, 0), parts):
        done_stage(part)

    total = tiny_total(1)
    like_all = total[1:2, :] / n_sim - total[0:1, :] / n_data
    like = like_all
    for z in range(1, n_st):
        like = jnp.where(st == z, pltpu.roll(like_all, 128 - z * group, 1), like)
    like_ref[...] = like

    for part in range(parts):
        for offset in range(1, n_ev):
            done_copy(part, offset, ev_slot[offset]).wait_recv()
        for index in range(n_ev):
            row, col = place(index)
            at = part * part_waves + col
            if col >= part_waves:
                at += waves - part_waves
            out_ref[row : row + 8, at : at + width] = done_in[part, index]

    for kind in range(2):
        tiny_core_copy(kind).wait_send()
        for offset in range(1, planes):
            tiny_plane_copy(kind, offset, plane).wait_send()
        for offset in range(1, n_st):
            tiny_st_copy(kind, offset, st).wait_send()
    for part in range(parts):
        core_copy(part).wait_send()
        for offset in range(1, planes):
            plane_copy(part, offset).wait_send()
        for offset in range(1, n_st):
            st_copy(part, offset).wait_send()
        for offset in range(1, n_ev):
            done_copy(part, offset, slot).wait_send()


def solution(mesh):
    n_ev = mesh.shape["ev"]
    n_st = mesh.shape["st"]
    n_dev = n_ev * n_st
    planes = n_ev // 2
    dma = pltpu.SemaphoreType.DMA
    vmem = pltpu.VMEM
    smem = pltpu.SMEM

    def shards(
        amplitudes, event_mass, data_rows, wave_shape, pole_mass, pole_width, coefficients, background
    ):
        rows, wide = amplitudes.shape
        waves = wide // 2
        starts = coefficients.shape[0]
        shapes = pole_mass.shape[0]
        group = starts // n_st
        parts = 4
        while (group // 8) * (wide // parts // 128) % n_ev:
            parts //= 2
        width = group * wide // (8 * n_ev * parts)
        blocks = rows // BLOCK
        piece = (8, width)
        gradient, like = pl.pallas_call(
            functools.partial(fit_kernel, n_ev, n_st, parts),
            in_specs=[pl.BlockSpec(memory_space=pltpu.HBM)] * 8,
            out_specs=[pl.BlockSpec(memory_space=pltpu.VMEM)] * 2,
            out_shape=[
                jax.ShapeDtypeStruct((group, wide), F32),
                jax.ShapeDtypeStruct((1, 128), F32),
            ],
            scratch_shapes=[
                smem((1,), jnp.int32),
                smem((shapes,), F32),
                smem((shapes,), F32),
                vmem((rows, wide), BF16),
                vmem((blocks, 1, BLOCK), F32),
                vmem((1, waves), jnp.int32),
                vmem((starts, wide), F32),
                vmem((1, starts), F32),
                vmem((wide, 2 * starts), BF16),
                vmem((8, waves), F32),
                vmem((8, waves), F32),
                vmem((BLOCK, 128), F32),
                vmem((8, 128), F32),
                vmem((blocks, 2 * starts, BLOCK), F32),
                vmem((2 * starts, rows), BF16),
                vmem((2, 3, 8, 128), F32),
                vmem((2, 8, 128), F32),
                vmem((2, planes, 8, 128), F32),
                vmem((2, n_st, 8, 128), F32),
                vmem((parts, 2, planes, n_st, *piece), F32),
                vmem((parts, planes, n_st, *piece), F32),
                vmem((parts, planes, n_st, *piece), F32),
                vmem((parts, planes, n_st, *piece), F32),
                vmem((parts, n_st, *piece), F32),
                vmem((parts, n_st, *piece), F32),
                vmem((parts, *piece), F32),
                vmem((parts, n_ev, *piece), F32),
                dma((7,)),
                dma((blocks,)),
                dma((2, planes + n_st)),
                dma((2, 1 + planes + n_st)),
                dma((parts,)),
                dma((parts,)),
                dma((parts, planes)),
                dma((parts, planes)),
                dma((parts, n_st)),
                dma((parts, n_st)),
                dma((parts, n_ev)),
                dma((parts, n_ev)),
            ],
            compiler_params=pltpu.CompilerParams(
                collective_id=0, has_side_effects=True, vmem_limit_bytes=40 * 1024 * 1024
            ),
            name="fit_all",
        )(
            data_rows,
            pole_mass,
            pole_width,
            amplitudes,
            event_mass.reshape(blocks, 1, BLOCK),
            wave_shape.reshape(1, waves),
            coefficients,
            background.reshape(1, starts),
        )
        return gradient, like[0, :group]

    return jax.shard_map(
        shards,
        mesh=mesh,
        in_specs=(P(("ev", "st"), None), P(("ev", "st")), P(("ev", "st")), P(), P(), P(), P(), P()),
        out_specs=(P("st", None), P("st")),
        check_vma=False,
    )
```

```python
import functools

import jax
import jax.numpy as jnp
from jax import lax
from jax.experimental import pallas as pl
from jax.experimental.pallas import tpu as pltpu
from jax.sharding import PartitionSpec as P

BLOCK = 512
ROWS = 16
LANES = 256
MESH = pl.DeviceIdType.MESH
F32 = jnp.float32
BF16 = jnp.bfloat16


def fit_kernel(
    n_ev,
    n_st,
    parts,
    limit_hbm,
    pole_mass_hbm,
    pole_width_hbm,
    amp_hbm,
    mass_hbm,
    wave_hbm,
    coef_hbm,
    back_hbm,
    out_ref,
    like_ref,
    limit_ref,
    pole_mass_ref,
    pole_width_ref,
    amp_ref,
    mass_ref,
    wave_ref,
    coef_ref,
    back_ref,
    mix,
    square,
    inverse,
    mass2,
    sums,
    raw,
    weights,
    tiny,
    tiny_core,
    tiny_plane,
    tiny_st,
    mine,
    core_in,
    plane_sum,
    plane_in,
    st_sum,
    st_in,
    done,
    done_in,
    load_sem,
    amp_sem,
    tiny_send,
    tiny_recv,
    core_send,
    core_recv,
    plane_send,
    plane_recv,
    st_send,
    st_recv,
    done_send,
    done_recv,
):
    ev = lax.axis_index("ev")
    st = lax.axis_index("st")
    n_dev = n_ev * n_st
    planes = n_ev // 2
    core = lax.rem(ev, 2)
    plane = lax.div(ev, 2)
    rows, wide = amp_ref.shape
    waves = wide // 2
    starts = back_ref.shape[1]
    group = starts // n_st
    events = rows * n_dev
    blocks = rows // BLOCK
    scale = waves ** (-0.5)
    width = mine.shape[-1]
    part_waves = waves // parts
    per = 2 * part_waves // width

    partner = (ev + 1 - 2 * core, st)
    plane_at = [lax.rem(plane + offset, planes) for offset in range(planes)]
    plane_to = [(2 * at + core, st) for at in plane_at]
    st_at = [lax.rem(st + offset, n_st) for offset in range(n_st)]
    ev_at = [lax.rem(ev + offset, n_ev) for offset in range(n_ev)]

    barrier = pltpu.get_barrier_semaphore()
    for offset in range(1, n_ev):
        pl.semaphore_signal(barrier, inc=1, device_id=(ev_at[offset], st), device_id_type=MESH)
    for offset in range(1, n_st):
        pl.semaphore_signal(barrier, inc=1, device_id=(ev, st_at[offset]), device_id_type=MESH)

    loads = [
        pltpu.make_async_copy(src, dst, load_sem.at[index])
        for index, (src, dst) in enumerate(
            [
                (coef_hbm, coef_ref),
                (wave_hbm, wave_ref),
                (limit_hbm, limit_ref),
                (pole_mass_hbm, pole_mass_ref),
                (pole_width_hbm, pole_width_ref),
                (mass_hbm, mass_ref),
                (back_hbm, back_ref),
            ]
        )
    ]
    for load in loads:
        load.start()

    def fetch(index):
        here = pl.ds(pl.multiple_of(index * BLOCK, BLOCK), BLOCK)
        return pltpu.make_async_copy(amp_hbm.at[here, :], amp_ref.at[here, :], amp_sem.at[index])

    for index in range(blocks):
        fetch(index).start()

    for load in loads:
        load.wait()
    limit = limit_ref[0]
    which = wave_ref[...]
    peak = jnp.zeros(which.shape, F32)
    center = jnp.zeros(which.shape, F32)
    for k in range(pole_mass_ref.shape[0]):
        mass_k = pole_mass_ref[k]
        peak = jnp.where(which == k, mass_k * pole_width_ref[k], peak)
        center = jnp.where(which == k, mass_k * mass_k, center)
    square[...] = jnp.broadcast_to(center, square.shape)
    inverse[...] = jnp.broadcast_to(1.0 / peak, inverse.shape)
    coef_real = coef_ref[:, :waves].T
    coef_imag = coef_ref[:, waves:].T
    mix[:waves, :starts] = coef_real.astype(BF16)
    mix[:waves, starts:] = coef_imag.astype(BF16)
    mix[waves:, :starts] = (-coef_imag).astype(BF16)
    mix[waves:, starts:] = coef_real.astype(BF16)
    sums[...] = jnp.zeros_like(sums)

    def tiny_copy(kind, stage, dst, send, recv, to):
        return pltpu.make_async_remote_copy(
            src_ref=tiny.at[kind, stage],
            dst_ref=dst,
            send_sem=tiny_send.at[kind, send],
            recv_sem=tiny_recv.at[kind, recv],
            device_id=to,
            device_id_type=MESH,
        )

    def tiny_core_copy(kind):
        return tiny_copy(kind, 0, tiny_core.at[kind], 0, 0, partner)

    def tiny_plane_copy(kind, offset, at):
        return tiny_copy(kind, 1, tiny_plane.at[kind, at], offset, 1 + at, plane_to[offset])

    def tiny_st_copy(kind, offset, at):
        return tiny_copy(
            kind,
            2,
            tiny_st.at[kind, at],
            planes + offset,
            1 + planes + at,
            (ev, st_at[offset]),
        )

    def tiny_core_stage(kind, value):
        tiny[kind, 0] = value
        tiny_core_copy(kind).start()

    def tiny_plane_stage(kind):
        tiny_core_copy(kind).wait_recv()
        value = tiny[kind, 0] + tiny_core[kind]
        tiny[kind, 1] = value
        for offset in range(1, planes):
            tiny_plane_copy(kind, offset, plane).start()
        tiny_plane[kind, plane] = value

    def tiny_st_stage(kind):
        for offset in range(1, planes):
            tiny_plane_copy(kind, offset, plane_at[offset]).wait_recv()
        value = tiny_plane[kind, 0]
        for index in range(1, planes):
            value = value + tiny_plane[kind, index]
        tiny[kind, 2] = value
        for offset in range(1, n_st):
            tiny_st_copy(kind, offset, st).start()
        tiny_st[kind, st] = value

    def tiny_total(kind):
        for offset in range(1, n_st):
            tiny_st_copy(kind, offset, st_at[offset]).wait_recv()
        value = tiny_st[kind, 0]
        for index in range(1, n_st):
            value = value + tiny_st[kind, index]
        return value

    def block_step(step, carry):
        first = pl.multiple_of(step * BLOCK, BLOCK)
        fetch(step).wait()

        @pl.when(step == 1)
        def _():
            pl.semaphore_wait(barrier, n_ev + n_st - 2)
            tiny_core_stage(0, jnp.full((8, 128), limit, jnp.int32).astype(F32))

        @pl.when(step == 2)
        def _():
            tiny_plane_stage(0)

        @pl.when(step == 3)
        def _():
            tiny_st_stage(0)

        mass = mass_ref[step]
        mass2[...] = jnp.broadcast_to(mass * mass, (128, BLOCK)).T

        def dress(index, carry):
            row = pl.multiple_of(index * ROWS, ROWS)
            here = pl.ds(pl.multiple_of(first + row, ROWS), ROWS)
            m2 = mass2[pl.ds(row, ROWS), :]
            m2 = jnp.concatenate([m2] * (LANES // 128), 1)
            for col in range(0, waves, LANES):
                real_cols = pl.ds(col, LANES)
                imag_cols = pl.ds(waves + col, LANES)
                sq = jnp.concatenate([square[:, real_cols]] * (ROWS // 8), 0)
                inv = jnp.concatenate([inverse[:, real_cols]] * (ROWS // 8), 0)
                u = (sq - m2) * inv
                denom = u * u + 1.0
                guess = pl.reciprocal(denom, approx=True)
                r = guess * (2.0 - denom * guess)
                amp_real = amp_ref[here, real_cols].astype(F32)
                amp_imag = amp_ref[here, imag_cols].astype(F32)
                amp_ref[here, real_cols] = ((amp_real * u - amp_imag) * r).astype(BF16)
                amp_ref[here, imag_cols] = ((amp_imag * u + amp_real) * r).astype(BF16)
            return carry

        lax.fori_loop(0, BLOCK // ROWS, dress, 0, unroll=4)

        dressed = amp_ref[pl.ds(first, BLOCK), :]
        value = jnp.dot(dressed, mix[...], preferred_element_type=F32) * scale
        val_real = value[:, :starts]
        val_imag = value[:, starts:]
        intensity = val_real * val_real + val_imag * val_imag + back_ref[...]
        is_data = first + lax.broadcasted_iota(jnp.int32, (BLOCK, starts), 0) < limit
        sums[0:1, :] += jnp.sum(jnp.where(is_data, jnp.log(intensity), 0.0), 0, keepdims=True)
        sums[1:2, :] += jnp.sum(jnp.where(is_data, 0.0, intensity), 0, keepdims=True)
        factor = jnp.where(is_data, -2.0 / intensity, 2.0)
        raw[step] = jnp.concatenate([factor * val_real, factor * val_imag], 1).T
        return carry

    lax.fori_loop(0, blocks, block_step, 0)

    tiny_core_stage(1, sums[...])
    n_data = tiny_total(0)[0:1, :]
    n_sim = events - n_data
    ratio = jnp.broadcast_to((n_sim / n_data)[:, 0:1], (2 * starts, BLOCK))
    final = jnp.broadcast_to((waves * scale / n_sim)[:, 0:1], (8, width))

    def scale_step(step, carry):
        first = step * BLOCK
        is_data = first + lax.broadcasted_iota(jnp.int32, (2 * starts, BLOCK), 1) < limit
        w = raw[step]
        here = pl.ds(pl.multiple_of(first, BLOCK), BLOCK)
        weights[:, here] = jnp.where(is_data, w * ratio, w).astype(BF16)
        return carry

    lax.fori_loop(0, blocks, scale_step, 0)

    def place(index):
        return 8 * (index // per), width * (index % per)

    def core_copy(part):
        return pltpu.make_async_remote_copy(
            src_ref=mine.at[part, 1 - core],
            dst_ref=core_in.at[part],
            send_sem=core_send.at[part],
            recv_sem=core_recv.at[part],
            device_id=partner,
            device_id_type=MESH,
        )

    def plane_copy(part, offset):
        to = plane_at[offset]
        return pltpu.make_async_remote_copy(
            src_ref=plane_sum.at[part, to],
            dst_ref=plane_in.at[part, offset],
            send_sem=plane_send.at[part, offset],
            recv_sem=plane_recv.at[part, offset],
            device_id=plane_to[offset],
            device_id_type=MESH,
        )

    def st_copy(part, offset):
        to = st_at[offset]
        return pltpu.make_async_remote_copy(
            src_ref=st_sum.at[part, to],
            dst_ref=st_in.at[part, offset],
            send_sem=st_send.at[part, offset],
            recv_sem=st_recv.at[part, offset],
            device_id=(ev, to),
            device_id_type=MESH,
        )

    def done_copy(part, offset, slot):
        return pltpu.make_async_remote_copy(
            src_ref=done.at[part],
            dst_ref=done_in.at[part, slot],
            send_sem=done_send.at[part, offset],
            recv_sem=done_recv.at[part, slot],
            device_id=(ev_at[offset], st),
            device_id_type=MESH,
        )

    slot = core * planes + plane
    ev_slot = [lax.rem(at, 2) * planes + lax.div(at, 2) for at in ev_at]

    def make_part(part):
        real_cols = pl.ds(part * part_waves, part_waves)
        imag_cols = pl.ds(waves + part * part_waves, part_waves)
        by_real = jnp.dot(weights[...], amp_ref[:, real_cols], preferred_element_type=F32)
        by_imag = jnp.dot(weights[...], amp_ref[:, imag_cols], preferred_element_type=F32)
        grad = jnp.concatenate(
            [by_real[:starts] + by_imag[starts:], by_real[starts:] - by_imag[:starts]], 1
        )
        for c in range(2):
            for p in range(planes):
                row, col = place(c * planes + p)
                for z in range(n_st):
                    at = z * group + row
                    mine[part, c, p, z] = grad[at : at + 8, col : col + width] * final
        core_copy(part).start()

    def plane_stage(part):
        core_copy(part).wait_recv()
        plane_sum[part] = mine[part, core] + core_in[part]
        for offset in range(1, planes):
            plane_copy(part, offset).start()

    def st_stage(part):
        total = plane_sum[part, plane]
        for offset in range(1, planes):
            plane_copy(part, offset).wait_recv()
            total = total + plane_in[part, offset]
        st_sum[part] = total
        for offset in range(1, n_st):
            st_copy(part, offset).start()

    def done_stage(part):
        total = st_sum[part, st]
        for offset in range(1, n_st):
            st_copy(part, offset).wait_recv()
            total = total + st_in[part, offset]
        done[part] = total
        for offset in range(1, n_ev):
            done_copy(part, offset, slot).start()
        done_in[part, slot] = total

    for part in range(parts):
        make_part(part)
        if part >= 1:
            plane_stage(part - 1)
        if part >= 3:
            st_stage(part - 3)
        if part == 0:
            tiny_plane_stage(1)
        if part == 1:
            tiny_st_stage(1)
    if parts >= 3:
        st_stage(parts - 3)
    plane_stage(parts - 1)
    for part in range(max(parts - 2, 0)):
        done_stage(part)
    if parts >= 2:
        st_stage(parts - 2)
    st_stage(parts - 1)
    for part in range(max(parts - 2, 0), parts):
        done_stage(part)

    total = tiny_total(1)
    like_all = total[1:2, :] / n_sim - total[0:1, :] / n_data
    like = like_all
    for z in range(1, n_st):
        like = jnp.where(st == z, pltpu.roll(like_all, 128 - z * group, 1), like)
    like_ref[...] = like

    for part in range(parts):
        for offset in range(1, n_ev):
            done_copy(part, offset, ev_slot[offset]).wait_recv()
        for index in range(n_ev):
            row, col = place(index)
            at = part * part_waves + col
            if col >= part_waves:
                at += waves - part_waves
            out_ref[row : row + 8, at : at + width] = done_in[part, index]

    for kind in range(2):
        tiny_core_copy(kind).wait_send()
        for offset in range(1, planes):
            tiny_plane_copy(kind, offset, plane).wait_send()
        for offset in range(1, n_st):
            tiny_st_copy(kind, offset, st).wait_send()
    for part in range(parts):
        core_copy(part).wait_send()
        for offset in range(1, planes):
            plane_copy(part, offset).wait_send()
        for offset in range(1, n_st):
            st_copy(part, offset).wait_send()
        for offset in range(1, n_ev):
            done_copy(part, offset, slot).wait_send()


def solution(mesh):
    n_ev = mesh.shape["ev"]
    n_st = mesh.shape["st"]
    n_dev = n_ev * n_st
    planes = n_ev // 2
    dma = pltpu.SemaphoreType.DMA
    vmem = pltpu.VMEM
    smem = pltpu.SMEM

    def shards(
        amplitudes, event_mass, data_rows, wave_shape, pole_mass, pole_width, coefficients, background
    ):
        rows, wide = amplitudes.shape
        waves = wide // 2
        starts = coefficients.shape[0]
        shapes = pole_mass.shape[0]
        group = starts // n_st
        parts = 4
        while (group // 8) * (wide // parts // 128) % n_ev:
            parts //= 2
        width = group * wide // (8 * n_ev * parts)
        blocks = rows // BLOCK
        piece = (8, width)
        gradient, like = pl.pallas_call(
            functools.partial(fit_kernel, n_ev, n_st, parts),
            in_specs=[pl.BlockSpec(memory_space=pltpu.HBM)] * 8,
            out_specs=[pl.BlockSpec(memory_space=pltpu.VMEM)] * 2,
            out_shape=[
                jax.ShapeDtypeStruct((group, wide), F32),
                jax.ShapeDtypeStruct((1, 128), F32),
            ],
            scratch_shapes=[
                smem((1,), jnp.int32),
                smem((shapes,), F32),
                smem((shapes,), F32),
                vmem((rows, wide), BF16),
                vmem((blocks, 1, BLOCK), F32),
                vmem((1, waves), jnp.int32),
                vmem((starts, wide), F32),
                vmem((1, starts), F32),
                vmem((wide, 2 * starts), BF16),
                vmem((8, waves), F32),
                vmem((8, waves), F32),
                vmem((BLOCK, 128), F32),
                vmem((8, 128), F32),
                vmem((blocks, 2 * starts, BLOCK), F32),
                vmem((2 * starts, rows), BF16),
                vmem((2, 3, 8, 128), F32),
                vmem((2, 8, 128), F32),
                vmem((2, planes, 8, 128), F32),
                vmem((2, n_st, 8, 128), F32),
                vmem((parts, 2, planes, n_st, *piece), F32),
                vmem((parts, planes, n_st, *piece), F32),
                vmem((parts, planes, n_st, *piece), F32),
                vmem((parts, planes, n_st, *piece), F32),
                vmem((parts, n_st, *piece), F32),
                vmem((parts, n_st, *piece), F32),
                vmem((parts, *piece), F32),
                vmem((parts, n_ev, *piece), F32),
                dma((7,)),
                dma((blocks,)),
                dma((2, planes + n_st)),
                dma((2, 1 + planes + n_st)),
                dma((parts,)),
                dma((parts,)),
                dma((parts, planes)),
                dma((parts, planes)),
                dma((parts, n_st)),
                dma((parts, n_st)),
                dma((parts, n_ev)),
                dma((parts, n_ev)),
            ],
            compiler_params=pltpu.CompilerParams(
                collective_id=0, has_side_effects=True, vmem_limit_bytes=40 * 1024 * 1024
            ),
            name="fit_all",
        )(
            data_rows,
            pole_mass,
            pole_width,
            amplitudes,
            event_mass.reshape(blocks, 1, BLOCK),
            wave_shape.reshape(1, waves),
            coefficients,
            background.reshape(1, starts),
        )
        return gradient, like[0, :group]

    return jax.shard_map(
        shards,
        mesh=mesh,
        in_specs=(P(("ev", "st"), None), P(("ev", "st")), P(("ev", "st")), P(), P(), P(), P(), P()),
        out_specs=(P("st", None), P("st")),
        check_vma=False,
    )
```
